256 devices in a mesh: row: 16 (over z, core), col: 16 (over x, y).
Axes of the slice: x: 4, y: 4, z: 8, core: 2. Of those that a mesh axis runs over, the one named last changes fastest.
Arguments:
- f_blocks: bfloat16 [32768, 8192], P('row', 'col'), may hold values from -0.25 to 0.25
- block_cols: int32 [512, 128], P('row', 'col'), may hold values from 0 to 23, as said below
- block_counts: int32 [512, 16], P('row', 'col'), may hold values from 1 to 8, as said below
- p_matrix: bfloat16 [24576, 8192], P('row', 'col'), may hold values from -6 to 6
Outputs:
- product: bfloat16 [32768, 8192], P('row', 'col')
The draws below stay inside these ranges and needn't reach their ends.
Inputs may be any that keep to these rules, and one draw needn't show every extreme that they name: `block_cols`: within one block row of one stored tile the 8 listed block columns are distinct, padded slots included. `block_counts`: some block row of every stored tile is full.
All inputs are finite; a program needn't handle non-finite values.
Results may differ from the reference program's by a relative error of at most 0.001.
Values may be sent and summed in bfloat16 or wider, within the bound.
A program may use at most 64 MiB of HBM per device.

```python
import jax
import jax.numpy as jnp
from jax import lax

BLOCK = 64
ROW_BLK = 32
K_BLK = 24
COL_BLK = 8
SLOTS = 8
NR_BLK = 512
NK_BLK = 384
NC_BLK = 128
N_ROW = 16
N_COL = 16


def draw_block_cols(key, part):
    scores = jax.random.randint(jax.random.fold_in(key, 11), (NR_BLK * N_COL, K_BLK), 0, 1 << 20)
    scores = scores * K_BLK + jnp.arange(K_BLK, dtype=jnp.int32)[None, :]
    order = jnp.argsort(scores, axis=1).astype(jnp.int32)
    return order[:, :SLOTS].reshape(NR_BLK, N_COL * SLOTS)


def draw_block_counts(key, part):
    counts = jax.random.randint(jax.random.fold_in(key, 23), (NR_BLK, N_COL), 1, SLOTS + 1)
    rows = jnp.arange(NR_BLK, dtype=jnp.int32)[:, None]
    return jnp.where(rows % ROW_BLK == 0, jnp.int32(SLOTS), counts).astype(jnp.int32)


def steps_of(key, shape, cuts, low, high):
    factor_of = 1.0
    for position, shards_of in cuts:
        steps = jax.random.uniform(jax.random.fold_in(jax.random.fold_in(key, 6), position), (shards_of,), jnp.float32, low / len(cuts), high / len(cuts))
        factor_of = factor_of * jnp.repeat(jnp.exp(steps), shape[position] // shards_of).reshape((-1,) + (1,) * (len(shape) - 1 - position))
    return factor_of


def centred(own_key, shape, scale, reach, pieces=(), held_as=jnp.bfloat16):
    result = jax.random.normal(own_key, shape, jnp.float32) * scale
    if len(pieces) > 0:
        result = steps_of(own_key, shape, pieces, -0.22, 0.18) * result
    return jnp.clip(result, min=-reach, max=reach).astype(held_as)


def setup_inputs(seed: int = 0) -> dict:
    key_of = jax.random.split(jax.random.key(seed), 5)
    f_blocks = centred(key_of[0], (NR_BLK * BLOCK, SLOTS * N_COL * BLOCK), (BLOCK * SLOTS) ** -0.5, 0.25, ((0, 16), (1, 16)))
    block_cols = draw_block_cols(jax.random.fold_in(key_of[4], 71), 0)
    block_counts = draw_block_counts(jax.random.fold_in(key_of[4], 71), 0)
    p_matrix = centred(key_of[3], (NK_BLK * BLOCK, NC_BLK * BLOCK), 1.0, 6.0, ((0, 16), (1, 16)))
    return {"f_blocks": f_blocks, "block_cols": block_cols, "block_counts": block_counts, "p_matrix": p_matrix}


def tile_term(f_blocks, block_cols, block_counts, p_matrix, i, j, s):
    g = (j + s) % N_COL
    h = (i + s) % N_ROW
    blocks = lax.dynamic_slice(f_blocks, ((i * ROW_BLK * BLOCK).astype(jnp.int32), (g * SLOTS * BLOCK).astype(jnp.int32)), (ROW_BLK * BLOCK, SLOTS * BLOCK))
    cols = lax.dynamic_slice(block_cols, ((i * ROW_BLK).astype(jnp.int32), (g * SLOTS).astype(jnp.int32)), (ROW_BLK, SLOTS))
    counts = lax.dynamic_slice(block_counts, ((i * ROW_BLK).astype(jnp.int32), g.astype(jnp.int32)), (ROW_BLK, 1))
    live = lax.broadcasted_iota(jnp.int32, (ROW_BLK, SLOTS), 1) < counts
    blocks = blocks.astype(jnp.float32).reshape(ROW_BLK, BLOCK, SLOTS, BLOCK)
    blocks = jnp.where(live[:, None, :, None], blocks, jnp.float32(0.0))
    tile = lax.dynamic_slice(p_matrix, ((h * K_BLK * BLOCK).astype(jnp.int32), (j * COL_BLK * BLOCK).astype(jnp.int32)), (K_BLK * BLOCK, COL_BLK * BLOCK))
    tile = tile.astype(jnp.float32).reshape(K_BLK, BLOCK, COL_BLK * BLOCK)
    picked = tile[cols]
    return jnp.einsum("rakb,rkbc->rac", blocks, picked).reshape(ROW_BLK * BLOCK, COL_BLK * BLOCK)


def reference(f_blocks, block_cols, block_counts, p_matrix):
    def one_tile(index):
        i = index // N_COL
        j = index % N_COL
        first = tile_term(f_blocks, block_cols, block_counts, p_matrix, i, j, 0)
        second = tile_term(f_blocks, block_cols, block_counts, p_matrix, i, j, 1)
        return (first + second).astype(jnp.bfloat16)

    tiles = lax.map(one_tile, jnp.arange(N_ROW * N_COL, dtype=jnp.int32))
    tiles = tiles.reshape(N_ROW, N_COL, ROW_BLK * BLOCK, COL_BLK * BLOCK)
    return tiles.transpose(0, 2, 1, 3).reshape(NR_BLK * BLOCK, NC_BLK * BLOCK)
```

```python
import functools

import jax
import jax.numpy as jnp
from jax import lax
from jax.experimental import pallas as pl
from jax.experimental.pallas import tpu as pltpu
from jax.sharding import PartitionSpec as P

EDGE = 64
CHUNK = 128
DIRECT = 12
RELAY = 4
P_STEP = 6
MESH = pl.DeviceIdType.MESH


def kernel(
    f_hbm, cols_h, cnt_h, p_hbm, out_hbm,
    cols_s, cnt_s, f_own, p_own, f_rx, hop1, hop2, p_rx, acc, outbuf,
    cols_rv, cnt_rv, cols_rs, cnt_rs,
    d_send, d_recv, r_send, r_recv, p_send, p_recv, m_send, m_recv, l_sem, o_sem,
):
    rows, width = f_hbm.shape
    slots = width // EDGE
    per = CHUNK // EDGE
    i = lax.axis_index("row")
    j = lax.axis_index("col")
    n_row = lax.axis_size("row")
    n_col = lax.axis_size("col")
    x, y = lax.div(j, 4), lax.rem(j, 4)
    to_direct = lax.rem(j + n_col - 1, n_col)
    from_direct = lax.rem(j + 1, n_col)
    to_ring = x * 4 + lax.rem(y + 1, 4)
    from_ring = x * 4 + lax.rem(y + 3, 4)
    nx = n_col // 4
    is3 = lax.div(y, 3)
    is2 = lax.div(y + 1, 3) - is3
    to_last = lax.rem(x + nx - is2, nx) * 4 + lax.rem(y + 1, 4)
    from_last = lax.rem(x + is3, nx) * 4 + lax.rem(y + 3, 4)
    to_p = lax.rem(i + n_row - 1, n_row)
    from_p = lax.rem(i + 1, n_row)

    own = [
        pltpu.make_async_copy(p_hbm, p_own, l_sem.at[0]),
        pltpu.make_async_copy(f_hbm, f_own, l_sem.at[1]),
        pltpu.make_async_copy(cols_h, cols_s, l_sem.at[4]),
        pltpu.make_async_copy(cnt_h, cnt_s, l_sem.at[5]),
    ]
    for copy in own:
        copy.start()

    barrier = pltpu.get_barrier_semaphore()
    for source in (from_direct, from_ring, from_last):
        pl.semaphore_signal(barrier, inc=1, device_id=(i, source), device_id_type=MESH)
    pl.semaphore_signal(barrier, inc=1, device_id=(from_p, j), device_id_type=MESH)
    pl.semaphore_wait(barrier, 4)

    def send(src, dst, ssem, rsem, target):
        return pltpu.make_async_remote_copy(
            src_ref=src, dst_ref=dst, send_sem=ssem, recv_sem=rsem,
            device_id=target, device_id_type=MESH,
        )

    meta = [
        send(cols_h, cols_rv, m_send.at[0], m_recv.at[0], (i, to_direct)),
        send(cnt_h, cnt_rv, m_send.at[1], m_recv.at[1], (i, to_direct)),
    ]
    p_copy = send(p_hbm, p_rx, p_send, p_recv, (to_p, j))
    direct = [
        send(f_hbm.at[pl.ds(k * CHUNK, CHUNK)], f_rx.at[pl.ds(k * CHUNK, CHUNK)],
             d_send.at[k], d_recv.at[k], (i, to_direct))
        for k in range(DIRECT)
    ]
    relay = []
    for k in range(3 * RELAY):
        hop, c = k // RELAY, k % RELAY
        part = pl.ds((DIRECT + c) * CHUNK, CHUNK)
        src = (f_hbm.at[part], hop1.at[c], hop2.at[c])[hop]
        dst = (hop1.at[c], hop2.at[c], f_rx.at[part])[hop]
        target = (to_ring, to_ring, to_last)[hop]
        relay.append(send(src, dst, r_send.at[k], r_recv.at[k], (i, target)))

    p_copy.start()
    for k in range(RELAY):
        direct[k].start()
        relay[k].start()
    for k in range(RELAY, DIRECT):
        direct[k].start()
    for copy in meta:
        copy.start()

    def term(f_ref, p_ref, cols, cnt, r):
        lhs = f_ref[pl.ds(pl.multiple_of(r * EDGE, EDGE), EDGE), :]
        lane = lax.broadcasted_iota(jnp.int32, lhs.shape, 1)
        lhs = jnp.where(lane < cnt[0, r] * EDGE, lhs, jnp.zeros_like(lhs))
        rhs = jnp.concatenate(
            [p_ref[cols[s, r]] for s in range(slots)],
            axis=0,
        )
        return jnp.dot(lhs, rhs, preferred_element_type=jnp.float32)

    for copy in own:
        copy.wait()

    @pl.loop(0, rows // EDGE)
    def _(r):
        acc[pl.ds(pl.multiple_of(r * EDGE, EDGE), EDGE), :] = term(f_own, p_own, cols_s, cnt_s, r)

    outs = {}

    def second(c):
        @pl.loop(c * per, (c + 1) * per)
        def _(r):
            part = pl.ds(pl.multiple_of(r * EDGE, EDGE), EDGE)
            total = acc[part, :] + term(f_rx, p_rx, cols_rs, cnt_rs, r)
            outbuf[part, :] = total.astype(outbuf.dtype)

        part = pl.ds(c * CHUNK, CHUNK)
        outs[c] = pltpu.make_async_copy(outbuf.at[part], out_hbm.at[part], o_sem.at[c])
        outs[c].start()

    done = 0
    for k in range(DIRECT):
        relay[k].wait_recv()
        if k < 2 * RELAY:
            relay[k + RELAY].start()
        direct[k].wait_recv()
        if k == P_STEP:
            for copy in meta:
                copy.wait()
            small = [
                pltpu.make_async_copy(cols_rv, cols_rs, l_sem.at[2]),
                pltpu.make_async_copy(cnt_rv, cnt_rs, l_sem.at[3]),
            ]
            for copy in small:
                copy.start()
            for copy in small:
                copy.wait()
            p_copy.wait()
        if k >= P_STEP:
            upto = k + 1 if k >= P_STEP + 2 else min(k + 1, done + 3)
            for c in range(done, upto):
                second(c)
            done = upto
            if k >= 2 * RELAY:
                second(DIRECT + k - 2 * RELAY)
    for copy in direct:
        copy.wait_send()
    for copy in relay:
        copy.wait_send()
    for copy in outs.values():
        copy.wait()


def body(f_blocks, block_cols, block_counts, p_matrix):
    rows, width = f_blocks.shape
    depth, wide = p_matrix.shape
    cols = block_cols.T
    counts = block_counts.T
    dma = pltpu.SemaphoreType.DMA
    any_spec = pl.BlockSpec(memory_space=pl.ANY)
    hbm = pl.BlockSpec(memory_space=pltpu.HBM)
    return pl.pallas_call(
        kernel,
        out_shape=jax.ShapeDtypeStruct((rows, wide), jnp.bfloat16),
        in_specs=[hbm, hbm, hbm, hbm],
        out_specs=any_spec,
        scratch_shapes=[
            pltpu.SMEM(cols.shape, jnp.int32),
            pltpu.SMEM(counts.shape, jnp.int32),
            pltpu.VMEM((rows, width), jnp.bfloat16),
            pltpu.VMEM((depth // EDGE, EDGE, wide), jnp.bfloat16),
            pltpu.VMEM((rows, width), jnp.bfloat16),
            pltpu.VMEM((RELAY, CHUNK, width), jnp.bfloat16),
            pltpu.VMEM((RELAY, CHUNK, width), jnp.bfloat16),
            pltpu.VMEM((depth // EDGE, EDGE, wide), jnp.bfloat16),
            pltpu.VMEM((rows, wide), jnp.float32),
            pltpu.VMEM((rows, wide), jnp.bfloat16),
            pltpu.VMEM(cols.shape, jnp.int32),
            pltpu.VMEM(counts.shape, jnp.int32),
            pltpu.SMEM(cols.shape, jnp.int32),
            pltpu.SMEM(counts.shape, jnp.int32),
            dma((DIRECT,)), dma((DIRECT,)),
            dma((3 * RELAY,)), dma((3 * RELAY,)),
            dma, dma,
            dma((2,)), dma((2,)),
            dma((6,)),
            dma((DIRECT + RELAY,)),
        ],
        compiler_params=pltpu.CompilerParams(
            collective_id=0, has_side_effects=True, vmem_limit_bytes=60000000
        ),
    )(f_blocks, cols, counts, p_matrix.reshape(depth // EDGE, EDGE, wide))


def solution(mesh):
    return jax.shard_map(
        body,
        mesh=mesh,
        in_specs=(P("row", "col"), P("row", "col"), P("row", "col"), P("row", "col")),
        out_specs=P("row", "col"),
        check_vma=False,
    )
```

```python
import jax
import jax.numpy as jnp
from jax import lax
from jax.experimental import pallas as pl
from jax.experimental.pallas import tpu as pltpu
from jax.sharding import PartitionSpec as P

EDGE = 64
DIRECT = (128,) * 11 + (64, 64)
RELAY = (128, 128, 128, 64, 64)
P_TIME = 0.5
LAG = 0.12
SIDE = 4
MESH = pl.DeviceIdType.MESH


def starts(sizes, base=0):
    out = []
    for size in sizes:
        out.append(base)
        base += size
    return out


def kernel(
    f_hbm, cols_h, cnt_h, p_hbm, out_hbm,
    cols_s, cnt_s, f_own, p_own, f_rx, hop1, hop2, landed, p_rx, acc, out_ref,
    cols_rv, cnt_rv, cols_rs, cnt_rs,
    d_send, d_recv, r_send, r_recv, x_send, x_recv, p_send, p_recv, m_send, m_recv, l_sem, o_sem,
):
    rows, width = f_hbm.shape
    slots = width // EDGE
    split = sum(DIRECT)
    n_d, n_r = len(DIRECT), len(RELAY)
    d_at, r_at = starts(DIRECT), starts(RELAY)
    i = lax.axis_index("row")
    j = lax.axis_index("col")
    n_row = lax.axis_size("row")
    n_col = lax.axis_size("col")
    nx = n_col // SIDE
    x, y = lax.div(j, SIDE), lax.rem(j, SIDE)
    to_direct = lax.rem(j + n_col - 1, n_col)
    from_direct = lax.rem(j + 1, n_col)
    to_ring = x * SIDE + lax.rem(y + 1, SIDE)
    from_ring = x * SIDE + lax.rem(y + SIDE - 1, SIDE)
    to_x = lax.rem(x + nx - 1, nx) * SIDE + y
    from_x = lax.rem(x + 1, nx) * SIDE + y
    to_p = lax.rem(i + n_row - 1, n_row)
    from_p = lax.rem(i + 1, n_row)
    turn = lax.div(y + 1, SIDE - 1) - lax.div(y, SIDE - 1)

    own = [
        pltpu.make_async_copy(p_hbm, p_own, l_sem.at[0]),
        pltpu.make_async_copy(f_hbm, f_own, l_sem.at[1]),
        pltpu.make_async_copy(cols_h, cols_s, l_sem.at[4]),
        pltpu.make_async_copy(cnt_h, cnt_s, l_sem.at[5]),
    ]
    barrier = pltpu.get_barrier_semaphore()
    for source in (from_direct, from_ring, from_x):
        pl.semaphore_signal(barrier, inc=1, device_id=(i, source), device_id_type=MESH)
    pl.semaphore_signal(barrier, inc=1, device_id=(from_p, j), device_id_type=MESH)
    for copy in own:
        copy.start()
    pl.semaphore_wait(barrier, 4)

    def send(src, dst, ssem, rsem, target):
        return pltpu.make_async_remote_copy(
            src_ref=src, dst_ref=dst, send_sem=ssem, recv_sem=rsem,
            device_id=target, device_id_type=MESH,
        )

    meta = [
        send(cols_h, cols_rv, m_send.at[0], m_recv.at[0], (i, to_direct)),
        send(cnt_h, cnt_rv, m_send.at[1], m_recv.at[1], (i, to_direct)),
    ]
    p_copy = send(p_hbm, p_rx, p_send, p_recv, (to_p, j))
    direct = [
        send(f_hbm.at[pl.ds(at, size)], f_rx.at[pl.ds(at, size)],
             d_send.at[k], d_recv.at[k], (i, to_direct))
        for k, (at, size) in enumerate(zip(d_at, DIRECT))
    ]
    relay = []
    for hop in range(3):
        for k, (at, size) in enumerate(zip(r_at, RELAY)):
            part = pl.ds(at, size)
            src = (f_hbm.at[pl.ds(split + at, size)], hop1.at[part], hop2.at[turn, part])[hop]
            dst = (hop1.at[part], hop2.at[0, part], landed.at[part])[hop]
            e = hop * n_r + k
            relay.append(send(src, dst, r_send.at[e], r_recv.at[e], (i, to_ring)))
    cross = [
        send(hop2.at[0, pl.ds(at, size)], hop2.at[1, pl.ds(at, size)],
             x_send.at[k], x_recv.at[k], (i, to_x))
        for k, (at, size) in enumerate(zip(r_at, RELAY))
    ]

    for copy in meta:
        copy.start()
    for k in range(n_d):
        direct[k].start()
        if k < n_r:
            relay[k].start()
        if k == 0:
            p_copy.start()
    def term(lhs, p_ref, cols, cnt, r):
        lane = lax.broadcasted_iota(jnp.int32, lhs.shape, 1)
        lhs = jnp.where(lane < cnt[0, r] * EDGE, lhs, jnp.zeros_like(lhs))
        rhs = jnp.concatenate([p_ref[cols[s, r]] for s in range(slots)], axis=0)
        return jnp.dot(lhs, rhs, preferred_element_type=jnp.float32)

    def span(r):
        return pl.ds(pl.multiple_of(r * EDGE, EDGE), EDGE)

    for copy in own:
        copy.wait()

    @pl.loop(0, rows // EDGE)
    def _(r):
        acc[span(r), :] = term(f_own[span(r), :], p_own, cols_s, cnt_s, r)

    first_late = split // EDGE

    outs = []

    def put(lo, hi):
        part = pl.ds(lo * EDGE, (hi - lo) * EDGE)
        outs.append(pltpu.make_async_copy(out_ref.at[part], out_hbm.at[part], o_sem.at[lo]))
        outs[-1].start()

    def second_direct(lo, hi):
        @pl.loop(lo, hi)
        def _(r):
            total = acc[span(r), :] + term(f_rx[span(r), :], p_rx, cols_rs, cnt_rs, r)
            out_ref[span(r), :] = total.astype(out_ref.dtype)

        put(lo, hi)

    def second_late(lo, hi):
        @pl.loop(lo, hi)
        def _(r):
            lhs = landed[span(r - first_late), :]
            total = acc[span(r), :] + term(lhs, p_rx, cols_rs, cnt_rs, r)
            out_ref[span(r), :] = total.astype(out_ref.dtype)

        put(lo, hi)

    events = [((at + size) / split, 1, k) for k, (at, size) in enumerate(zip(d_at, DIRECT))]
    events += [
        ((hop * (rows - split) + at + size) / split, 0, hop * n_r + k)
        for hop in range(3) for k, (at, size) in enumerate(zip(r_at, RELAY))
    ]
    events += [
        ((rows - split + at + size) / split + LAG, 2, k)
        for k, (at, size) in enumerate(zip(r_at, RELAY))
    ]
    done = ready = 0
    late = []
    have_p = False
    for time, kind, k in sorted(events):
        if kind == 1:
            direct[k].wait_recv()
            ready = (d_at[k] + DIRECT[k]) // EDGE
        elif kind == 2:

            @pl.when(turn == 1)
            def _():
                cross[k].wait_recv()

            relay[2 * n_r + k].start()
        else:
            relay[k].wait_recv()
            if k < n_r:
                relay[k + n_r].start()
            elif k < 2 * n_r:

                @pl.when(turn == 1)
                def _():
                    cross[k - n_r].start()
            else:
                late.append(k - 2 * n_r)
        if time >= P_TIME and not have_p:
            have_p = True
            for copy in meta:
                copy.wait()
            small = [
                pltpu.make_async_copy(cols_rv, cols_rs, l_sem.at[2]),
                pltpu.make_async_copy(cnt_rv, cnt_rs, l_sem.at[3]),
            ]
            for copy in small:
                copy.start()
            for copy in small:
                copy.wait()
            p_copy.wait()
        if have_p and kind == 1:
            upto = min(ready, done + 6)
            second_direct(done, upto)
            done = upto
            while late:
                c = late.pop(0)
                lo = (split + r_at[c]) // EDGE
                second_late(lo, lo + RELAY[c] // EDGE)
    if done < ready:
        second_direct(done, ready)
    for c in late:
        lo = (split + r_at[c]) // EDGE
        second_late(lo, lo + RELAY[c] // EDGE)
    for copy in direct + relay:
        copy.wait_send()

    @pl.when(turn == 1)
    def _():
        for copy in cross:
            copy.wait_send()

    for copy in outs:
        copy.wait()


def body(f_blocks, block_cols, block_counts, p_matrix):
    rows, width = f_blocks.shape
    depth, wide = p_matrix.shape
    cols = block_cols.T
    counts = block_counts.T
    tiles = (depth // EDGE, EDGE, wide)
    late = sum(RELAY)
    dma = pltpu.SemaphoreType.DMA
    any_spec = pl.BlockSpec(memory_space=pl.ANY)
    return pl.pallas_call(
        kernel,
        out_shape=jax.ShapeDtypeStruct((rows, wide), jnp.bfloat16),
        in_specs=[any_spec] * 4,
        out_specs=any_spec,
        scratch_shapes=[
            pltpu.SMEM(cols.shape, jnp.int32),
            pltpu.SMEM(counts.shape, jnp.int32),
            pltpu.VMEM((rows, width), jnp.bfloat16),
            pltpu.VMEM(tiles, jnp.bfloat16),
            pltpu.VMEM((sum(DIRECT), width), jnp.bfloat16),
            pltpu.VMEM((late, width), jnp.bfloat16),
            pltpu.VMEM((2, late, width), jnp.bfloat16),
            pltpu.VMEM((late, width), jnp.bfloat16),
            pltpu.VMEM(tiles, jnp.bfloat16),
            pltpu.VMEM((rows, wide), jnp.float32),
            pltpu.VMEM((rows, wide), jnp.bfloat16),
            pltpu.VMEM(cols.shape, jnp.int32),
            pltpu.VMEM(counts.shape, jnp.int32),
            pltpu.SMEM(cols.shape, jnp.int32),
            pltpu.SMEM(counts.shape, jnp.int32),
            dma((len(DIRECT),)), dma((len(DIRECT),)),
            dma((3 * len(RELAY),)), dma((3 * len(RELAY),)),
            dma((len(RELAY),)), dma((len(RELAY),)),
            dma, dma,
            dma((2,)), dma((2,)),
            dma((6,)),
            dma((rows // EDGE,)),
        ],
        compiler_params=pltpu.CompilerParams(
            collective_id=0, has_side_effects=True, vmem_limit_bytes=63000000
        ),
    )(f_blocks, cols, counts, p_matrix.reshape(tiles))


def solution(mesh):
    return jax.shard_map(
        body,
        mesh=mesh,
        in_specs=(P("row", "col"), P("row", "col"), P("row", "col"), P("row", "col")),
        out_specs=P("row", "col"),
        check_vma=False,
    )
```

```python
import jax
import jax.numpy as jnp
from jax import lax
from jax.experimental import pallas as pl
from jax.experimental.pallas import tpu as pltpu
from jax.sharding import PartitionSpec as P

EDGE = 64
DIRECT = (128,) * 11 + (64, 64)
RELAY = (128, 128, 128, 64, 64)
P_TIME = 0.5
LAG = 0.12
SIDE = 4
MESH = pl.DeviceIdType.MESH


def starts(sizes, base=0):
    out = []
    for size in sizes:
        out.append(base)
        base += size
    return out


def kernel(
    f_hbm, cols_h, cnt_h, p_hbm, out_ref,
    cols_s, cnt_s, f_own, p_own, f_rx, hop1, hop2, landed, p_rx, acc,
    cols_rv, cnt_rv, cols_rs, cnt_rs,
    d_send, d_recv, r_send, r_recv, x_send, x_recv, p_send, p_recv, m_send, m_recv, l_sem,
):
    rows, width = f_hbm.shape
    slots = width // EDGE
    split = sum(DIRECT)
    n_d, n_r = len(DIRECT), len(RELAY)
    d_at, r_at = starts(DIRECT), starts(RELAY)
    i = lax.axis_index("row")
    j = lax.axis_index("col")
    n_row = lax.axis_size("row")
    n_col = lax.axis_size("col")
    nx = n_col // SIDE
    x, y = lax.div(j, SIDE), lax.rem(j, SIDE)
    to_direct = lax.rem(j + n_col - 1, n_col)
    from_direct = lax.rem(j + 1, n_col)
    to_ring = x * SIDE + lax.rem(y + 1, SIDE)
    from_ring = x * SIDE + lax.rem(y + SIDE - 1, SIDE)
    to_x = lax.rem(x + nx - 1, nx) * SIDE + y
    from_x = lax.rem(x + 1, nx) * SIDE + y
    to_p = lax.rem(i + n_row - 1, n_row)
    from_p = lax.rem(i + 1, n_row)
    turn = lax.div(y + 1, SIDE - 1) - lax.div(y, SIDE - 1)

    own = [
        pltpu.make_async_copy(p_hbm, p_own, l_sem.at[0]),
        pltpu.make_async_copy(f_hbm, f_own, l_sem.at[1]),
        pltpu.make_async_copy(cols_h, cols_s, l_sem.at[4]),
        pltpu.make_async_copy(cnt_h, cnt_s, l_sem.at[5]),
    ]
    barrier = pltpu.get_barrier_semaphore()
    for source in (from_direct, from_ring, from_x):
        pl.semaphore_signal(barrier, inc=1, device_id=(i, source), device_id_type=MESH)
    pl.semaphore_signal(barrier, inc=1, device_id=(from_p, j), device_id_type=MESH)
    for copy in own:
        copy.start()
    pl.semaphore_wait(barrier, 4)

    def send(src, dst, ssem, rsem, target):
        return pltpu.make_async_remote_copy(
            src_ref=src, dst_ref=dst, send_sem=ssem, recv_sem=rsem,
            device_id=target, device_id_type=MESH,
        )

    meta = [
        send(cols_h, cols_rv, m_send.at[0], m_recv.at[0], (i, to_direct)),
        send(cnt_h, cnt_rv, m_send.at[1], m_recv.at[1], (i, to_direct)),
    ]
    p_copy = send(p_hbm, p_rx, p_send, p_recv, (to_p, j))
    direct = [
        send(f_hbm.at[pl.ds(at, size)], f_rx.at[pl.ds(at, size)],
             d_send.at[k], d_recv.at[k], (i, to_direct))
        for k, (at, size) in enumerate(zip(d_at, DIRECT))
    ]
    relay = []
    for hop in range(3):
        for k, (at, size) in enumerate(zip(r_at, RELAY)):
            part = pl.ds(at, size)
            src = (f_hbm.at[pl.ds(split + at, size)], hop1.at[part], hop2.at[turn, part])[hop]
            dst = (hop1.at[part], hop2.at[0, part], landed.at[part])[hop]
            e = hop * n_r + k
            relay.append(send(src, dst, r_send.at[e], r_recv.at[e], (i, to_ring)))
    cross = [
        send(hop2.at[0, pl.ds(at, size)], hop2.at[1, pl.ds(at, size)],
             x_send.at[k], x_recv.at[k], (i, to_x))
        for k, (at, size) in enumerate(zip(r_at, RELAY))
    ]

    for copy in meta:
        copy.start()
    for k in range(n_d):
        direct[k].start()
        if k < n_r:
            relay[k].start()
        if k == 0:
            p_copy.start()
    def term(lhs, p_ref, cols, cnt, r):
        lane = lax.broadcasted_iota(jnp.int32, lhs.shape, 1)
        lhs = jnp.where(lane < cnt[0, r] * EDGE, lhs, jnp.zeros_like(lhs))
        rhs = jnp.concatenate([p_ref[cols[s, r]] for s in range(slots)], axis=0)
        return jnp.dot(lhs, rhs, preferred_element_type=jnp.float32)

    def span(r):
        return pl.ds(pl.multiple_of(r * EDGE, EDGE), EDGE)

    for copy in own:
        copy.wait()

    @pl.loop(0, rows // EDGE)
    def _(r):
        acc[span(r), :] = term(f_own[span(r), :], p_own, cols_s, cnt_s, r)

    first_late = split // EDGE

    def second_direct(lo, hi):
        @pl.loop(lo, hi)
        def _(r):
            total = acc[span(r), :] + term(f_rx[span(r), :], p_rx, cols_rs, cnt_rs, r)
            out_ref[span(r), :] = total.astype(out_ref.dtype)

    def second_late(lo, hi):
        @pl.loop(lo, hi)
        def _(r):
            lhs = landed[span(r - first_late), :]
            total = acc[span(r), :] + term(lhs, p_rx, cols_rs, cnt_rs, r)
            out_ref[span(r), :] = total.astype(out_ref.dtype)

    events = [((at + size) / split, 1, k) for k, (at, size) in enumerate(zip(d_at, DIRECT))]
    events += [
        ((hop * (rows - split) + at + size) / split, 0, hop * n_r + k)
        for hop in range(3) for k, (at, size) in enumerate(zip(r_at, RELAY))
    ]
    events += [
        ((rows - split + at + size) / split + LAG, 2, k)
        for k, (at, size) in enumerate(zip(r_at, RELAY))
    ]
    done = ready = 0
    late = []
    have_p = False
    for time, kind, k in sorted(events):
        if kind == 1:
            direct[k].wait_recv()
            ready = (d_at[k] + DIRECT[k]) // EDGE
        elif kind == 2:

            @pl.when(turn == 1)
            def _():
                cross[k].wait_recv()

            relay[2 * n_r + k].start()
        else:
            relay[k].wait_recv()
            if k < n_r:
                relay[k + n_r].start()
            elif k < 2 * n_r:

                @pl.when(turn == 1)
                def _():
                    cross[k - n_r].start()
            else:
                late.append(k - 2 * n_r)
        if time >= P_TIME and not have_p:
            have_p = True
            for copy in meta:
                copy.wait()
            small = [
                pltpu.make_async_copy(cols_rv, cols_rs, l_sem.at[2]),
                pltpu.make_async_copy(cnt_rv, cnt_rs, l_sem.at[3]),
            ]
            for copy in small:
                copy.start()
            for copy in small:
                copy.wait()
            p_copy.wait()
        if have_p and kind == 1:
            upto = min(ready, done + 6)
            second_direct(done, upto)
            done = upto
            while late:
                c = late.pop(0)
                lo = (split + r_at[c]) // EDGE
                second_late(lo, lo + RELAY[c] // EDGE)
    if done < ready:
        second_direct(done, ready)
    for c in late:
        lo = (split + r_at[c]) // EDGE
        second_late(lo, lo + RELAY[c] // EDGE)
    for copy in direct + relay:
        copy.wait_send()

    @pl.when(turn == 1)
    def _():
        for copy in cross:
            copy.wait_send()


def body(f_blocks, block_cols, block_counts, p_matrix):
    rows, width = f_blocks.shape
    depth, wide = p_matrix.shape
    cols = block_cols.T
    counts = block_counts.T
    tiles = (depth // EDGE, EDGE, wide)
    late = sum(RELAY)
    dma = pltpu.SemaphoreType.DMA
    any_spec = pl.BlockSpec(memory_space=pl.ANY)
    return pl.pallas_call(
        kernel,
        out_shape=pltpu.VMEM((rows, wide), jnp.bfloat16),
        in_specs=[any_spec] * 4,
        out_specs=pl.BlockSpec(memory_space=pltpu.VMEM),
        scratch_shapes=[
            pltpu.SMEM(cols.shape, jnp.int32),
            pltpu.SMEM(counts.shape, jnp.int32),
            pltpu.VMEM((rows, width), jnp.bfloat16),
            pltpu.VMEM(tiles, jnp.bfloat16),
            pltpu.VMEM((sum(DIRECT), width), jnp.bfloat16),
            pltpu.VMEM((late, width), jnp.bfloat16),
            pltpu.VMEM((2, late, width), jnp.bfloat16),
            pltpu.VMEM((late, width), jnp.bfloat16),
            pltpu.VMEM(tiles, jnp.bfloat16),
            pltpu.VMEM((rows, wide), jnp.float32),
            pltpu.VMEM(cols.shape, jnp.int32),
            pltpu.VMEM(counts.shape, jnp.int32),
            pltpu.SMEM(cols.shape, jnp.int32),
            pltpu.SMEM(counts.shape, jnp.int32),
            dma((len(DIRECT),)), dma((len(DIRECT),)),
            dma((3 * len(RELAY),)), dma((3 * len(RELAY),)),
            dma((len(RELAY),)), dma((len(RELAY),)),
            dma, dma,
            dma((2,)), dma((2,)),
            dma((6,)),
        ],
        compiler_params=pltpu.CompilerParams(
            collective_id=0, has_side_effects=True, vmem_limit_bytes=63000000
        ),
    )(*(pltpu.with_memory_space_constraint(a, pltpu.HBM) for a in (f_blocks, cols, counts, p_matrix.reshape(tiles))))


def solution(mesh):
    return jax.shard_map(
        body,
        mesh=mesh,
        in_specs=(P("row", "col"), P("row", "col"), P("row", "col"), P("row", "col")),
        out_specs=P("row", "col"),
        check_vma=False,
    )
```

```python
import jax
import jax.numpy as jnp
from jax import lax
from jax.experimental import pallas as pl
from jax.experimental.pallas import tpu as pltpu
from jax.sharding import PartitionSpec as P

EDGE = 64
DIRECT = (128,) * 11 + (64, 64)
RELAY = (128, 128, 128, 64, 64)
EXTRA = DIRECT[-1]
P_TIME = 0.55
LAG = 0.12
SHIFT = 0.2
SIDE = 4
MESH = pl.DeviceIdType.MESH


def starts(sizes, base=0):
    out = []
    for size in sizes:
        out.append(base)
        base += size
    return out


def kernel(
    f_hbm, cols_h, cnt_h, p_hbm, out_ref,
    cols_s, cnt_s, f_own, p_own, f_rx, hop1, hop2, landed, p_rx, acc,
    cols_rv, cnt_rv, cols_rs, cnt_rs,
    d_send, d_recv, r_send, r_recv, x_send, x_recv, p_send, p_recv, m_send, m_recv, l_sem, ready,
):
    rows, width = f_hbm.shape
    slots = width // EDGE
    split = sum(DIRECT)
    n_d, n_r = len(DIRECT), len(RELAY)
    d_at, r_at = starts(DIRECT), starts(RELAY)
    i = lax.axis_index("row")
    j = lax.axis_index("col")
    n_row = lax.axis_size("row")
    n_col = lax.axis_size("col")
    nx = n_col // SIDE
    x, y = lax.div(j, SIDE), lax.rem(j, SIDE)
    to_direct = lax.rem(j + n_col - 1, n_col)
    from_direct = lax.rem(j + 1, n_col)
    to_ring = x * SIDE + lax.rem(y + 1, SIDE)
    from_ring = x * SIDE + lax.rem(y + SIDE - 1, SIDE)
    to_x = lax.rem(x + nx - 1, nx) * SIDE + y
    from_x = lax.rem(x + 1, nx) * SIDE + y
    to_p = lax.rem(i + n_row - 1, n_row)
    from_p = lax.rem(i + 1, n_row)
    turn = lax.div(y + 1, SIDE - 1) - lax.div(y, SIDE - 1)

    own = [
        pltpu.make_async_copy(p_hbm, p_own, l_sem.at[0]),
        pltpu.make_async_copy(f_hbm, f_own, l_sem.at[1]),
        pltpu.make_async_copy(cols_h, cols_s, l_sem.at[4]),
        pltpu.make_async_copy(cnt_h, cnt_s, l_sem.at[5]),
    ]
    barrier = pltpu.get_barrier_semaphore()

    def tell(when, sem, device):
        @pl.when(when)
        def _():
            pl.semaphore_signal(sem, inc=1, device_id=device, device_id_type=MESH)

    def after(when, sem):
        @pl.when(when)
        def _():
            pl.semaphore_wait(sem, 1)

    first_i, last_i = i == 0, i == n_row - 1
    first_y, last_y = y == 0, y == SIDE - 1
    turns = turn == 1
    first_x = jnp.logical_and(turns, x == 0)
    last_x = jnp.logical_and(turns, x == nx - 1)
    tell(jnp.logical_not(last_y), barrier, (i, to_ring))
    tell(first_y, barrier, (i, from_ring))
    tell(jnp.logical_not(last_y), barrier, (i, from_direct))
    tell(first_y, barrier, (i, to_direct))
    tell(jnp.logical_not(last_i), barrier, (from_p, j))
    tell(first_i, barrier, (to_p, j))
    tell(jnp.logical_and(turns, x != nx - 1), barrier, (i, from_x))
    tell(first_x, barrier, (i, to_x))
    tell(jnp.logical_and(i == 1, first_y), barrier, (to_p, j))
    for copy in own:
        copy.start()
    inner_y = 1 - lax.div(SIDE - 1 - y, SIDE - 1)
    edge_y = lax.div(y, SIDE - 1)
    inner_i = 1 - lax.div(n_row - 1 - i, n_row - 1)
    inner_x = 1 - lax.div(nx - 1 - x, nx - 1)
    expected = inner_i + lax.div(i, n_row - 1) + 2 * inner_y + 2 * edge_y
    expected = expected + turn * (inner_x + lax.div(x, nx - 1))
    expected = expected + (1 - inner_i) * (1 - inner_y)
    pl.semaphore_wait(barrier, expected)
    tell(jnp.logical_not(first_y), ready.at[0], (i, from_ring))
    tell(last_y, ready.at[1], (i, from_direct))
    tell(last_i, ready.at[2], (from_p, j))
    tell(last_x, ready.at[3], (i, from_x))

    def send(src, dst, ssem, rsem, target):
        return pltpu.make_async_remote_copy(
            src_ref=src, dst_ref=dst, send_sem=ssem, recv_sem=rsem,
            device_id=target, device_id_type=MESH,
        )

    meta = [
        send(cols_h, cols_rv, m_send.at[0], m_recv.at[0], (i, to_direct)),
        send(cnt_h, cnt_rv, m_send.at[1], m_recv.at[1], (i, to_direct)),
    ]
    p_copy = send(p_hbm, p_rx, p_send, p_recv, (to_p, j))
    direct = [
        send(f_hbm.at[pl.ds(at, size)], f_rx.at[pl.ds(at, size)],
             d_send.at[k], d_recv.at[k], (i, to_direct))
        for k, (at, size) in enumerate(zip(d_at, DIRECT))
    ]
    late_rows = sum(RELAY)
    parts = [(late_rows, EXTRA, d_at[-1])]
    parts += [(at, size, split + at) for at, size in zip(r_at, RELAY)]
    n_c = len(parts)

    def only(when, act):
        if when is None:
            act()
        else:
            pl.when(when)(act)

    def sender_of(e):
        return y == e // n_c if e % n_c == 0 else None

    def receiver_of(e):
        return y == e // n_c + 1 if e % n_c == 0 else None

    relay = []
    for hop in range(3):
        for k, (at, size, row) in enumerate(parts):
            part = pl.ds(at, size)
            src = (f_hbm.at[pl.ds(row, size)], hop1.at[part], hop2.at[turn, part])[hop]
            final = f_rx.at[pl.ds(row, size)] if k == 0 else landed.at[part]
            dst = (hop1.at[part], hop2.at[0, part], final)[hop]
            e = hop * n_c + k
            relay.append(send(src, dst, r_send.at[e], r_recv.at[e], (i, to_ring)))
    cross = [
        send(hop2.at[0, pl.ds(at, size)], hop2.at[1, pl.ds(at, size)],
             x_send.at[k], x_recv.at[k], (i, to_x))
        for k, (at, size, row) in enumerate(parts)
    ]

    def start_direct():
        for copy in meta + direct[:-1]:
            copy.start()

    pl.when(jnp.logical_not(first_y))(start_direct)
    pl.when(jnp.logical_not(first_y))(direct[-1].start)
    pl.when(jnp.logical_not(first_i))(p_copy.start)
    after(jnp.logical_not(last_y), ready.at[0])
    for k in range(n_c):
        only(sender_of(k), relay[k].start)
    after(first_y, ready.at[1])
    pl.when(first_y)(start_direct)
    after(first_i, ready.at[2])
    pl.when(first_i)(p_copy.start)
    after(first_x, ready.at[3])

    def term(lhs, p_ref, cols, cnt, r):
        lane = lax.broadcasted_iota(jnp.int32, lhs.shape, 1)
        lhs = jnp.where(lane < cnt[0, r] * EDGE, lhs, jnp.zeros_like(lhs))
        rhs = jnp.concatenate([p_ref[cols[s, r]] for s in range(slots)], axis=0)
        return jnp.dot(lhs, rhs, preferred_element_type=jnp.float32)

    def span(r):
        return pl.ds(pl.multiple_of(r * EDGE, EDGE), EDGE)

    for copy in own:
        copy.wait()

    @pl.loop(0, rows // EDGE)
    def _(r):
        acc[span(r), :] = term(f_own[span(r), :], p_own, cols_s, cnt_s, r)

    first_late = split // EDGE

    def second_direct(lo, hi):
        @pl.loop(lo, hi)
        def _(r):
            total = acc[span(r), :] + term(f_rx[span(r), :], p_rx, cols_rs, cnt_rs, r)
            out_ref[span(r), :] = total.astype(out_ref.dtype)

    def second_late(lo, hi):
        @pl.loop(lo, hi)
        def _(r):
            lhs = landed[span(r - first_late), :]
            total = acc[span(r), :] + term(lhs, p_rx, cols_rs, cnt_rs, r)
            out_ref[span(r), :] = total.astype(out_ref.dtype)

    events = []
    for k, (at, size) in enumerate(zip(d_at, DIRECT)):
        share = (at + size) / split
        events.append((share + SHIFT * (1 - share), 1, k))
    for k, (at, size, row) in enumerate(parts):
        end = (size if k == 0 else at + size) / split
        for hop in range(3):
            events.append((hop * late_rows / split + end, 0, hop * n_c + k))
        events.append((late_rows / split + end + LAG, 2, k))
    done = fresh = 0
    late = []
    have_p = False
    for time, kind, k in sorted(events):
        if kind == 1:
            only(None if k < n_d - 1 else jnp.logical_not(last_y), direct[k].wait_recv)
            fresh = (d_at[k] + DIRECT[k]) // EDGE
        elif kind == 2:
            pl.when(turns)(cross[k].wait_recv)
            only(sender_of(2 * n_c + k), relay[2 * n_c + k].start)
        elif k < 2 * n_c:

            def forward():
                relay[k].wait_recv()
                if k < n_c:
                    relay[k + n_c].start()
                else:
                    pl.when(turns)(cross[k - n_c].start)

            only(receiver_of(k), forward)
        else:
            only(receiver_of(k), relay[k].wait_recv)
            if k > 2 * n_c:
                late.append(k - 2 * n_c - 1)
        if time >= P_TIME and not have_p:
            have_p = True
            for copy in meta:
                copy.wait()
            small = [
                pltpu.make_async_copy(cols_rv, cols_rs, l_sem.at[2]),
                pltpu.make_async_copy(cnt_rv, cnt_rs, l_sem.at[3]),
            ]
            for copy in small:
                copy.start()
            for copy in small:
                copy.wait()
            p_copy.wait()
        if have_p and kind == 1:
            upto = min(fresh, done + 6)
            second_direct(done, upto)
            done = upto
            while late:
                c = late.pop(0)
                lo = (split + r_at[c]) // EDGE
                second_late(lo, lo + RELAY[c] // EDGE)
    if done < fresh:
        second_direct(done, fresh)
    for c in late:
        lo = (split + r_at[c]) // EDGE
        second_late(lo, lo + RELAY[c] // EDGE)
    for copy in direct[:-1]:
        copy.wait_send()
    pl.when(jnp.logical_not(first_y))(direct[-1].wait_send)
    for e in range(3 * n_c):
        only(sender_of(e), relay[e].wait_send)

    @pl.when(turn == 1)
    def _():
        for copy in cross:
            copy.wait_send()


def body(f_blocks, block_cols, block_counts, p_matrix):
    rows, width = f_blocks.shape
    depth, wide = p_matrix.shape
    cols = block_cols.T
    counts = block_counts.T
    tiles = (depth // EDGE, EDGE, wide)
    late = sum(RELAY)
    held = late + EXTRA
    n_c = len(RELAY) + 1
    dma = pltpu.SemaphoreType.DMA
    any_spec = pl.BlockSpec(memory_space=pl.ANY)
    return pl.pallas_call(
        kernel,
        out_shape=pltpu.VMEM((rows, wide), jnp.bfloat16),
        in_specs=[any_spec] * 4,
        out_specs=pl.BlockSpec(memory_space=pltpu.VMEM),
        scratch_shapes=[
            pltpu.SMEM(cols.shape, jnp.int32),
            pltpu.SMEM(counts.shape, jnp.int32),
            pltpu.VMEM((rows, width), jnp.bfloat16),
            pltpu.VMEM(tiles, jnp.bfloat16),
            pltpu.VMEM((sum(DIRECT), width), jnp.bfloat16),
            pltpu.VMEM((held, width), jnp.bfloat16),
            pltpu.VMEM((2, held, width), jnp.bfloat16),
            pltpu.VMEM((late, width), jnp.bfloat16),
            pltpu.VMEM(tiles, jnp.bfloat16),
            pltpu.VMEM((rows, wide), jnp.float32),
            pltpu.VMEM(cols.shape, jnp.int32),
            pltpu.VMEM(counts.shape, jnp.int32),
            pltpu.SMEM(cols.shape, jnp.int32),
            pltpu.SMEM(counts.shape, jnp.int32),
            dma((len(DIRECT),)), dma((len(DIRECT),)),
            dma((3 * n_c,)), dma((3 * n_c,)),
            dma((n_c,)), dma((n_c,)),
            dma, dma,
            dma((2,)), dma((2,)),
            dma((6,)),
            pltpu.SemaphoreType.REGULAR((4,)),
        ],
        compiler_params=pltpu.CompilerParams(
            collective_id=0, has_side_effects=True, vmem_limit_bytes=63000000
        ),
    )(*(pltpu.with_memory_space_constraint(a, pltpu.HBM) for a in (f_blocks, cols, counts, p_matrix.reshape(tiles))))


def solution(mesh):
    return jax.shard_map(
        body,
        mesh=mesh,
        in_specs=(P("row", "col"), P("row", "col"), P("row", "col"), P("row", "col")),
        out_specs=P("row", "col"),
        check_vma=False,
    )
```
